32 devices in a mesh: groups: 2 (over y), row: 4 (over z), col: 2 (over x), pole: 2 (over core).
Axes of the slice: x: 2, y: 2, z: 4, core: 2. Of those that a mesh axis runs over, the one named last changes fastest.
Arguments:
- inverse: bfloat16 [4, 2, 8192, 8192], P(('groups', 'pole'), None, 'row', 'col'), parts along dimension 0, may hold values from -6 to 6
- lower: bfloat16 [4, 8192, 2, 3, 256], P(('groups', 'pole'), ('col', 'row')), parts along dimension 0, may hold values from -0.0625 to 0.0625
- upper: bfloat16 [4, 8192, 2, 3, 256], P(('groups', 'pole'), ('row', 'col')), parts along dimension 0, may hold values from -0.0625 to 0.0625
- diag_inverse: bfloat16 [4, 3, 2, 256, 256], P(('groups', 'pole')), parts along dimension 0, may hold values from -6 to 6
- weights: float32 [4, 2], P(('groups', 'pole')), parts along dimension 0, may hold values from -4 to 4
- pattern: int32 [6, 16], P('groups'), parts along dimension 0, may hold values from 0 to 31, as said below
Outputs:
- column_density: float32 [16384, 3, 256], P(('groups', 'row', 'col', 'pole')), parts along dimension 0
- row_density: float32 [16384, 3, 256], P(('groups', 'col', 'row', 'pole')), parts along dimension 0
- diagonal_density: float32 [6, 256, 256], P('groups'), parts along dimension 0
The draws below stay inside these ranges and needn't reach their ends.
There are 2 independent parts, one for each index of `groups`. The reference program is written for one: setup_inputs(seed, part) draws one part's arguments, and reference() takes and returns one part's arrays. A program takes and returns all parts, laid end to end along the dimension named above; each array names one. Nothing has to cross between parts.
Inputs may be any that keep to these rules, and one draw needn't show every extreme that they name: `pattern`: each row names 16 different ancestor blocks, and the rows together name every ancestor block.
All inputs are finite; a program needn't handle non-finite values.
Results may differ from the reference program's by a relative error of at most 0.0003.
Values may be sent and summed in bfloat16 or wider, within the bound.
A program may use at most 192 MiB of HBM per device.

```python
import jax
import jax.numpy as jnp
from jax import lax

BW = 256
NB = 32
PAT = 16
SUPER = 3
ANC = 8192
POLES = 2


def draw_pattern(key, part):
    order = jax.random.permutation(jax.random.fold_in(key, 17), NB).astype(jnp.int32)
    supers = jnp.arange(SUPER, dtype=jnp.int32)[:, None]
    slots = jnp.arange(PAT, dtype=jnp.int32)[None, :]
    positions = (supers * PAT + slots) % NB
    return order[positions].astype(jnp.int32)


def levels(key, dims, shards, least, high):
    def one(axis_at, blocks):
        heights = jax.random.uniform(jax.random.fold_in(jax.random.fold_in(key, 6), axis_at), (blocks,), jnp.float32, least / len(shards), high / len(shards))
        return jnp.repeat(jnp.exp(heights), dims[axis_at] // blocks).reshape((-1,) + (1,) * (len(dims) - axis_at - 1))

    factor_of = one(*shards[0])
    for cut in shards[1:]:
        factor_of = factor_of * one(*cut)
    return factor_of


def normal_values(own_key, dims, deviation, most, split=(), kind=jnp.bfloat16):
    array = deviation * jax.random.normal(own_key, dims, jnp.float32)
    if split:
        array = array * levels(own_key, dims, split, -0.22, 0.18)
    return jnp.clip(array, -most, most).astype(kind)


def setup_inputs(seed: int = 0, part: int = 0) -> dict:
    splits = jax.random.split(jax.random.key(seed), 7)
    own_keys = jax.random.split(jax.random.fold_in(splits[6], part), 7)
    inverse = normal_values(own_keys[0], (POLES, 2, ANC, ANC), 1.0, 6.0, ((0, 2), (2, 4), (3, 2)))
    lower = normal_values(own_keys[1], (POLES, ANC, 2, SUPER, BW), (2 * PAT * BW) ** -0.5, 0.0625, ((0, 2), (1, 8)))
    upper = normal_values(own_keys[2], (POLES, ANC, 2, SUPER, BW), (2 * PAT * BW) ** -0.5, 0.0625, ((0, 2), (1, 8)))
    diag_inverse = normal_values(own_keys[3], (POLES, SUPER, 2, BW, BW), 1.0, 6.0, ((0, 2),))
    weights = normal_values(own_keys[4], (POLES, 2), 1.0, 4.0, ((0, 2),), jnp.float32)
    pattern = draw_pattern(jax.random.fold_in(jax.random.fold_in(splits[6], part), 71), part)
    return dict(inverse=inverse, lower=lower, upper=upper, diag_inverse=diag_inverse, weights=weights, pattern=pattern)


def kept_rows(pattern):
    blocks = jnp.arange(ANC, dtype=jnp.int32) // BW
    hits = pattern[:, :, None] == blocks[None, None, :]
    return jnp.any(hits, axis=1)


def transposed_dot(left, right):
    return lax.dot_general(left, right, (((0,), (0,)), ((), ())), preferred_element_type=jnp.float32)


def reference(inverse, lower, upper, diag_inverse, weights, pattern):
    keep = jnp.transpose(kept_rows(pattern))[:, None, :, None]
    column_density = jnp.zeros((ANC, SUPER * BW), jnp.float32)
    row_density = jnp.zeros((ANC, SUPER * BW), jnp.float32)
    diagonal_density = jnp.zeros((SUPER, BW, BW), jnp.float32)
    highest = lax.Precision.HIGHEST
    for pole in range(POLES):
        real_inverse = inverse[pole, 0]
        imag_inverse = inverse[pole, 1]
        lower_kept = jnp.where(keep, lower[pole], jnp.zeros_like(lower[pole]))
        upper_kept = jnp.where(keep, upper[pole], jnp.zeros_like(upper[pole]))
        real_lower = lower_kept[:, 0].reshape(ANC, SUPER * BW)
        imag_lower = lower_kept[:, 1].reshape(ANC, SUPER * BW)
        real_upper = upper_kept[:, 0].reshape(ANC, SUPER * BW)
        imag_upper = upper_kept[:, 1].reshape(ANC, SUPER * BW)
        column_real = -(jnp.dot(real_inverse, real_lower, preferred_element_type=jnp.float32)
                        - jnp.dot(imag_inverse, imag_lower, preferred_element_type=jnp.float32))
        column_imag = -(jnp.dot(real_inverse, imag_lower, preferred_element_type=jnp.float32)
                        + jnp.dot(imag_inverse, real_lower, preferred_element_type=jnp.float32))
        row_real = -(transposed_dot(real_inverse, real_upper) - transposed_dot(imag_inverse, imag_upper))
        row_imag = -(transposed_dot(real_inverse, imag_upper) + transposed_dot(imag_inverse, real_upper))
        weight_real = weights[pole, 0]
        weight_imag = weights[pole, 1]
        column_density = column_density + weight_real * column_imag + weight_imag * column_real
        row_density = row_density + weight_real * row_imag + weight_imag * row_real
        zeta_real = row_real.reshape(ANC, SUPER, BW)
        zeta_imag = row_imag.reshape(ANC, SUPER, BW)
        lower_real = real_lower.astype(jnp.float32).reshape(ANC, SUPER, BW)
        lower_imag = imag_lower.astype(jnp.float32).reshape(ANC, SUPER, BW)
        prod_real = (jnp.einsum("nsa,nsb->sab", zeta_real, lower_real, precision=highest)
                     - jnp.einsum("nsa,nsb->sab", zeta_imag, lower_imag, precision=highest))
        prod_imag = (jnp.einsum("nsa,nsb->sab", zeta_real, lower_imag, precision=highest)
                     + jnp.einsum("nsa,nsb->sab", zeta_imag, lower_real, precision=highest))
        given = diag_inverse[pole].astype(jnp.float32)
        diag_real = given[:, 0] - prod_real
        diag_imag = given[:, 1] - prod_imag
        diagonal_density = diagonal_density + weight_real * diag_imag + weight_imag * diag_real
    return (column_density.reshape(ANC, SUPER, BW), row_density.reshape(ANC, SUPER, BW), diagonal_density)
```

```python
import functools

import jax
import jax.numpy as jnp
from jax import lax
from jax.experimental import pallas as pl
from jax.experimental.pallas import tpu as pltpu
from jax.sharding import PartitionSpec as P


def row_kernel(meta, weights, a_ref, u_ref, *rest):
    if len(rest) == 3:
        prev_ref, out_ref, acc = rest
    else:
        prev_ref = None
        out_ref, acc = rest
    k = pl.program_id(1)
    steps = pl.num_programs(1)
    supers, double, _ = acc.shape
    width = double // 2
    unit = a_ref.shape[1]
    poles, part = out_ref.shape[1], out_ref.shape[3]

    @pl.when(k == 0)
    def _():
        acc[...] = jnp.zeros_like(acc)

    for s in range(supers):
        @pl.when(meta[1 + k * supers + s] > 0)
        def _():
            acc[s] += jnp.dot(u_ref[k, s, :, :unit], a_ref[0], preferred_element_type=jnp.float32) + jnp.dot(
                u_ref[k, s, :, unit:], a_ref[1], preferred_element_type=jnp.float32
            )

    @pl.when(k == steps - 1)
    def _():
        for s in range(supers):
            value = -(weights[0] * acc[s, width:] + weights[1] * acc[s, :width])
            for p in range(poles):
                piece = value[:, p * part:(p + 1) * part]
                if prev_ref is not None:
                    piece = piece + prev_ref[0, p, s * width:(s + 1) * width, :]
                out_ref[0, p, s * width:(s + 1) * width, :] = piece


def row_call(meta, weights, inverse, factor, prev, n_row, n_pole):
    _, rows, cols = inverse.shape
    steps, supers, double, double_unit = factor.shape
    unit = double_unit // 2
    width = double // 2
    tile = cols // n_row
    block_out = (1, n_pole, supers * width, tile // n_pole)
    out_spec = pl.BlockSpec(block_out, lambda n, k, meta: (n, 0, 0, 0))
    in_specs = [
        pl.BlockSpec(memory_space=pltpu.SMEM),
        pl.BlockSpec((2, unit, tile), lambda n, k, meta: (0, meta[0] + k, n)),
        pl.BlockSpec(factor.shape, lambda n, k, meta: (0, 0, 0, 0)),
    ]
    operands = [meta, weights, inverse, factor]
    if prev is not None:
        in_specs.append(out_spec)
        operands.append(prev)
    return pl.pallas_call(
        row_kernel,
        out_shape=jax.ShapeDtypeStruct((n_row,) + block_out[1:], jnp.float32),
        grid_spec=pltpu.PrefetchScalarGridSpec(
            num_scalar_prefetch=1,
            grid=(n_row, steps),
            in_specs=in_specs,
            out_specs=out_spec,
            scratch_shapes=[pltpu.VMEM((supers, double, tile), jnp.float32)],
        ),
        compiler_params=pltpu.CompilerParams(vmem_limit_bytes=56 * 2**20),
        cost_estimate=pl.CostEstimate(
            flops=4 * steps * unit * cols * supers * double // 2 * 2, bytes_accessed=4 * steps * unit * cols, transcendentals=0
        ),
        name="row_product",
    )(*operands)


def column_kernel(pieces, meta, weights, a_ref, l_ref, *rest):
    u_refs = rest[:pieces]
    out_ref, diag_ref, acc = rest[pieces:]
    k = pl.program_id(0)
    steps = pl.num_programs(0)
    unit, double = l_ref.shape
    width = double // 2
    parts = u_refs[0].shape[0]
    base = 1 + steps

    @pl.when(k == 0)
    def _():
        acc[...] = jnp.zeros_like(acc)

    @pl.when(k < meta[0])
    def _():
        first = l_ref[...]
        second = jnp.concatenate([-first[:, width:], first[:, :width]], axis=1)
        acc[...] += jnp.dot(a_ref[0], first, preferred_element_type=jnp.float32) + jnp.dot(
            a_ref[1], second, preferred_element_type=jnp.float32
        )

    @pl.when(k == steps - 1)
    def _():
        real = acc[:, :width]
        imag = acc[:, width:]
        mixed = weights[0] * imag + weights[1] * real
        out_ref[...] = -mixed
        acc[:, width:] = weights[0] * real - weights[1] * imag
        acc[:, :width] = mixed
        diag_ref[...] = jnp.zeros_like(diag_ref)
        for i in range(pieces):
            for b in range(parts):
                @pl.when(meta[base + pieces + i * parts + b] > 0)
                def _():
                    start = pl.multiple_of(meta[base + i] + b * unit, unit)
                    value = acc[pl.ds(start, unit), :]
                    high = value.astype(jnp.bfloat16)
                    low = (value - high.astype(jnp.float32)).astype(jnp.bfloat16)
                    total = jnp.zeros(diag_ref.shape, jnp.float32)
                    for half in (high, low):
                        for c in range(2):
                            total += jnp.dot(
                                u_refs[i][b, 0, c * width:(c + 1) * width, :],
                                half[:, c * width:(c + 1) * width],
                                preferred_element_type=jnp.float32,
                            )
                    diag_ref[...] += total


def column_call(meta, weights, inverse, lower, factors, s):
    _, rows, cols = inverse.shape
    double = lower.shape[1]
    width = double // 2
    parts, supers, _, double_unit = factors[0].shape
    unit = double_unit // 2
    steps = cols // unit
    return pl.pallas_call(
        functools.partial(column_kernel, len(factors)),
        out_shape=(
            jax.ShapeDtypeStruct((rows, width), jnp.float32),
            jax.ShapeDtypeStruct((width, width), jnp.float32),
        ),
        grid_spec=pltpu.PrefetchScalarGridSpec(
            num_scalar_prefetch=1,
            grid=(steps,),
            in_specs=[
                pl.BlockSpec(memory_space=pltpu.SMEM),
                pl.BlockSpec((2, rows, unit), lambda k, meta: (0, 0, meta[1 + k])),
                pl.BlockSpec((unit, double), lambda k, meta: (meta[1 + k], 0)),
            ]
            + [pl.BlockSpec((parts, 1, double, unit), lambda k, meta: (0, s, 0, 0))] * len(factors),
            out_specs=(
                pl.BlockSpec((rows, width), lambda k, meta: (0, 0)),
                pl.BlockSpec((width, width), lambda k, meta: (0, 0)),
            ),
            scratch_shapes=[pltpu.VMEM((rows, double), jnp.float32)],
        ),
        compiler_params=pltpu.CompilerParams(vmem_limit_bytes=48 * 2**20),
        cost_estimate=pl.CostEstimate(
            flops=4 * rows * cols * double // 2, bytes_accessed=2 * rows * cols, transcendentals=0
        ),
        name="column_product",
    )(meta, weights, inverse, lower, *factors)


def shifted(array, axis, pairs):
    return lax.ppermute(array, axis, pairs)


def transposed_factor(piece, unit):
    rows, _, supers, width = piece.shape
    turned = jnp.transpose(piece.reshape(rows // unit, unit, 2, supers, width), (0, 3, 2, 4, 1))
    real = turned[:, :, 0]
    imag = turned[:, :, 1]
    return jnp.concatenate(
        [jnp.concatenate([real, -imag], axis=3), jnp.concatenate([imag, real], axis=3)], axis=2
    )


def body(inverse, lower, upper, diag_inverse, weights, pattern):
    n_row = lax.axis_size("row")
    n_col = lax.axis_size("col")
    n_pole = lax.axis_size("pole")
    z = lax.axis_index("row")
    x = lax.axis_index("col")
    pole = lax.axis_index("pole")
    _, local, _, supers, width = lower.shape
    inverse = inverse[0]
    _, rows, cols = inverse.shape
    unit = min(width, local)
    blocks = local // unit
    weights = weights[0]
    total_units = n_row * n_col * blocks
    owner = (lax.iota(jnp.int32, total_units) * unit) // width
    keep = jnp.any(pattern[:, :, None] == owner[None, None, :], axis=1).astype(jnp.int32)

    own_lower = jnp.transpose(lower[0], (2, 0, 1, 3)).reshape(supers, local, 2 * width)
    gathered = []
    for s in range(supers):
        forward = [own_lower[s]]
        backward = [own_lower[s]]
        for step in range(1, n_row):
            forward.append(shifted(forward[-1], "row", [(i, i + 1) for i in range(step - 1, n_row - 1)]))
            backward.append(shifted(backward[-1], "row", [(i, i - 1) for i in range(1, n_row - step + 1)]))
        full = jnp.zeros((n_row * local, 2 * width), lower.dtype)
        full = lax.dynamic_update_slice(full, own_lower[s], (z * local, 0))
        for d in range(1, n_row):
            piece = jnp.where(z >= d, forward[d], backward[n_row - d])
            full = lax.dynamic_update_slice(full, piece, (lax.rem(z - d + n_row, n_row) * local, 0))
        gathered.append(full)

    pieces = [upper[0]]
    for d in range(1, n_col):
        pieces.append(shifted(upper[0], "col", [(i, (i + d) % n_col) for i in range(n_col)]))
    row_total = None
    factors = []
    starts = []
    piece_keeps = []
    for d in range(n_col):
        origin = lax.rem(x - d + n_col, n_col)
        factor = transposed_factor(pieces[d], unit)
        factors.append(factor)
        starts.append(origin * local)
        piece_keep = lax.dynamic_slice(keep, (0, (z * n_col + origin) * blocks), (supers, blocks))
        piece_keeps.append(piece_keep)
        meta = jnp.concatenate([(origin * blocks)[None], jnp.transpose(piece_keep).reshape(-1)])
        row_total = row_call(meta, weights, inverse, factor, row_total, n_row, n_pole)

    swap = [(i, n_pole - 1 - i) for i in range(n_pole)]
    mine = lax.dynamic_index_in_dim(row_total, pole, 1, keepdims=False)
    other = lax.dynamic_index_in_dim(row_total, n_pole - 1 - pole, 1, keepdims=False)
    summed = mine + shifted(other, "pole", swap)
    ahead = None
    behind = None
    for step in range(1, n_row):
        chunk = lax.dynamic_index_in_dim(summed, jnp.clip(n_row - step + z, 0, n_row - 1), 0, keepdims=False)
        send = chunk if ahead is None else chunk + ahead
        ahead = shifted(send, "row", [(i, i + 1) for i in range(0, min(step, n_row - 1))])
        chunk = lax.dynamic_index_in_dim(summed, jnp.clip(step - n_row + z, 0, n_row - 1), 0, keepdims=False)
        send = chunk if behind is None else chunk + behind
        behind = shifted(send, "row", [(i, i - 1) for i in range(n_row - step, n_row)])
    row_density = lax.dynamic_index_in_dim(summed, z, 0, keepdims=False)
    if ahead is not None:
        row_density = row_density + ahead + behind
    row_density = jnp.transpose(row_density).reshape(-1, supers, width)

    slots = n_row * blocks
    col_keep = lax.dynamic_slice(keep, (0, x * slots), (supers, slots))
    columns = []
    diagonals = []
    first_device = jnp.logical_and(z == 0, x == 0)
    given = diag_inverse[0].astype(jnp.float32)
    own_term = weights[0] * given[:, 1] + weights[1] * given[:, 0]
    own_term = jnp.where(first_device, own_term, jnp.zeros_like(own_term))
    for s in range(supers):
        count = jnp.sum(col_keep[s])
        rank = jnp.cumsum(col_keep[s]) - 1
        slot = lax.iota(jnp.int32, slots)
        wanted = jnp.minimum(slot, jnp.maximum(count - 1, 0))
        hit = jnp.logical_and(rank[None, :] == wanted[:, None], col_keep[s][None, :] > 0)
        order = jnp.sum(jnp.where(hit, slot[None, :], 0), axis=1)
        meta = jnp.concatenate(
            [count[None], order, jnp.stack(starts)] + [piece_keep[s] for piece_keep in piece_keeps]
        ).astype(jnp.int32)
        part, diag = column_call(meta, weights, inverse, gathered[s], factors, s)
        part = part.reshape(n_col, n_pole, -1, width)
        mine = lax.dynamic_index_in_dim(part, pole, 1, keepdims=False)
        other = lax.dynamic_index_in_dim(part, n_pole - 1 - pole, 1, keepdims=False)
        half = mine + shifted(other, "pole", swap)
        column = lax.dynamic_index_in_dim(half, x, 0, keepdims=False)
        for d in range(1, n_col):
            send = lax.dynamic_index_in_dim(half, lax.rem(x + d, n_col), 0, keepdims=False)
            column = column + shifted(send, "col", [(i, (i + d) % n_col) for i in range(n_col)])
        columns.append(column)
        diagonals.append(diag + own_term[s])
    column_density = jnp.stack(columns, axis=1)
    diagonal_density = lax.psum(jnp.stack(diagonals), ("row", "col", "pole"))
    return (column_density, row_density, diagonal_density)


def solution(mesh):
    return jax.shard_map(
        body,
        mesh=mesh,
        in_specs=(
            P(("groups", "pole"), None, "row", "col"),
            P(("groups", "pole"), ("col", "row"), None, None, None),
            P(("groups", "pole"), ("row", "col"), None, None, None),
            P(("groups", "pole"), None, None, None, None),
            P(("groups", "pole"), None),
            P("groups", None),
        ),
        out_specs=(
            P(("groups", "row", "col", "pole"), None, None),
            P(("groups", "col", "row", "pole"), None, None),
            P("groups", None, None),
        ),
        check_vma=False,
    )
```

```python
import functools

import jax
import jax.numpy as jnp
from jax import lax
from jax.experimental import pallas as pl
from jax.experimental.pallas import tpu as pltpu
from jax.sharding import PartitionSpec as P


def row_kernel(meta, weights, a_ref, u_ref, *rest):
    if len(rest) == 3:
        prev_ref, out_ref, acc = rest
    else:
        prev_ref = None
        out_ref, acc = rest
    k = pl.program_id(1)
    steps = pl.num_programs(1)
    supers, double, _ = acc.shape
    width = double // 2
    poles, part = out_ref.shape[1], out_ref.shape[3]

    @pl.when(k == 0)
    def _():
        acc[...] = jnp.zeros_like(acc)

    for s in range(supers):
        @pl.when(meta[1 + k * supers + s] > 0)
        def _():
            real = u_ref[k, s, 0]
            imag = u_ref[k, s, 1]
            first = jnp.concatenate([real, imag], axis=0)
            second = jnp.concatenate([-imag, real], axis=0)
            acc[s] += jnp.dot(first, a_ref[0], preferred_element_type=jnp.float32) + jnp.dot(
                second, a_ref[1], preferred_element_type=jnp.float32
            )

    @pl.when(k == steps - 1)
    def _():
        for s in range(supers):
            value = -(weights[0] * acc[s, width:] + weights[1] * acc[s, :width])
            for p in range(poles):
                piece = value[:, p * part:(p + 1) * part]
                if prev_ref is not None:
                    piece = piece + prev_ref[0, p, s * width:(s + 1) * width, :]
                out_ref[0, p, s * width:(s + 1) * width, :] = piece


def row_call(meta, weights, inverse, factor, prev, n_row, n_pole):
    _, _, cols = inverse.shape
    steps, supers, _, width, unit = factor.shape
    double = 2 * width
    tile = cols // n_row
    block_out = (1, n_pole, supers * width, tile // n_pole)
    out_spec = pl.BlockSpec(block_out, lambda n, k, meta: (n, 0, 0, 0))
    in_specs = [
        pl.BlockSpec(memory_space=pltpu.SMEM),
        pl.BlockSpec((2, unit, tile), lambda n, k, meta: (0, meta[0] + k, n)),
        pl.BlockSpec(factor.shape, lambda n, k, meta: (0, 0, 0, 0, 0)),
    ]
    operands = [meta, weights, inverse, factor]
    if prev is not None:
        in_specs.append(out_spec)
        operands.append(prev)
    return pl.pallas_call(
        row_kernel,
        out_shape=jax.ShapeDtypeStruct((n_row,) + block_out[1:], jnp.float32),
        grid_spec=pltpu.PrefetchScalarGridSpec(
            num_scalar_prefetch=1,
            grid=(n_row, steps),
            in_specs=in_specs,
            out_specs=out_spec,
            scratch_shapes=[pltpu.VMEM((supers, double, tile), jnp.float32)],
        ),
        compiler_params=pltpu.CompilerParams(vmem_limit_bytes=56 * 2**20),
        cost_estimate=pl.CostEstimate(
            flops=4 * steps * unit * cols * supers * double // 2 * 2, bytes_accessed=4 * steps * unit * cols, transcendentals=0
        ),
        name="row_product",
    )(*operands)


def column_kernel(pieces, meta, weights, a_ref, l_ref, *rest):
    u_refs = rest[:pieces]
    out_ref, diag_ref, acc = rest[pieces:]
    k = pl.program_id(0)
    steps = pl.num_programs(0)
    unit, double = l_ref.shape
    width = double // 2
    parts = u_refs[0].shape[0]
    base = 1 + steps

    @pl.when(k == 0)
    def _():
        acc[...] = jnp.zeros_like(acc)

    @pl.when(k < meta[0])
    def _():
        first = l_ref[...]
        second = jnp.concatenate([-first[:, width:], first[:, :width]], axis=1)
        acc[...] += jnp.dot(a_ref[0], first, preferred_element_type=jnp.float32) + jnp.dot(
            a_ref[1], second, preferred_element_type=jnp.float32
        )

    @pl.when(k == steps - 1)
    def _():
        real = acc[:, :width]
        imag = acc[:, width:]
        mixed = weights[0] * imag + weights[1] * real
        out_ref[...] = -mixed
        acc[:, width:] = weights[0] * real - weights[1] * imag
        acc[:, :width] = mixed
        diag_ref[...] = jnp.zeros_like(diag_ref)
        for i in range(pieces):
            for b in range(parts):
                @pl.when(meta[base + pieces + i * parts + b] > 0)
                def _():
                    start = pl.multiple_of(meta[base + i] + b * unit, unit)
                    value = acc[pl.ds(start, unit), :]
                    high = value.astype(jnp.bfloat16)
                    low = (value - high.astype(jnp.float32)).astype(jnp.bfloat16)
                    total = jnp.zeros(diag_ref.shape, jnp.float32)
                    for half in (high, low):
                        for c in range(2):
                            total += jnp.dot(
                                u_refs[i][b, 0, c],
                                half[:, c * width:(c + 1) * width],
                                preferred_element_type=jnp.float32,
                            )
                    diag_ref[...] += total


def column_call(meta, weights, inverse, lower, factors, s):
    _, rows, cols = inverse.shape
    double = lower.shape[1]
    width = double // 2
    parts, _, _, _, unit = factors[0].shape
    steps = cols // unit
    return pl.pallas_call(
        functools.partial(column_kernel, len(factors)),
        out_shape=(
            jax.ShapeDtypeStruct((rows, width), jnp.float32),
            jax.ShapeDtypeStruct((width, width), jnp.float32),
        ),
        grid_spec=pltpu.PrefetchScalarGridSpec(
            num_scalar_prefetch=1,
            grid=(steps,),
            in_specs=[
                pl.BlockSpec(memory_space=pltpu.SMEM),
                pl.BlockSpec((2, rows, unit), lambda k, meta: (0, 0, meta[1 + k])),
                pl.BlockSpec((unit, double), lambda k, meta: (meta[1 + k], 0)),
            ]
            + [pl.BlockSpec((parts, 1, 2, width, unit), lambda k, meta: (0, s, 0, 0, 0))] * len(factors),
            out_specs=(
                pl.BlockSpec((rows, width), lambda k, meta: (0, 0)),
                pl.BlockSpec((width, width), lambda k, meta: (0, 0)),
            ),
            scratch_shapes=[pltpu.VMEM((rows, double), jnp.float32)],
        ),
        compiler_params=pltpu.CompilerParams(vmem_limit_bytes=48 * 2**20),
        cost_estimate=pl.CostEstimate(
            flops=4 * rows * cols * double // 2, bytes_accessed=2 * rows * cols, transcendentals=0
        ),
        name="column_product",
    )(meta, weights, inverse, lower, *factors)


def transposed_factor(piece, unit):
    rows, _, supers, width = piece.shape
    return jnp.transpose(piece.reshape(rows // unit, unit, 2, supers, width), (0, 3, 2, 4, 1))


def taken(array, index, axis):
    return lax.dynamic_index_in_dim(array, index, axis, keepdims=False)


def summed_everywhere(array, axes):
    if not axes:
        return array
    axis = axes[0]
    n = lax.axis_size(axis)
    me = lax.axis_index(axis)
    split = array.reshape((n, -1) + array.shape[1:])
    total = taken(split, me, 0)
    for d in range(1, n):
        pairs = [(i, (i + d) % n) for i in range(n)]
        total = total + lax.ppermute(taken(split, lax.rem(me + d, n), 0), axis, pairs)
    total = summed_everywhere(total, axes[1:])
    result = lax.dynamic_update_index_in_dim(jnp.zeros_like(split), total, me, 0)
    for d in range(1, n):
        pairs = [(i, (i + d) % n) for i in range(n)]
        got = lax.ppermute(total, axis, pairs)
        result = lax.dynamic_update_index_in_dim(result, got, lax.rem(me - d + n, n), 0)
    return result.reshape(array.shape)


def body(inverse, lower, upper, diag_inverse, weights, pattern):
    n_row = lax.axis_size("row")
    n_col = lax.axis_size("col")
    n_pole = lax.axis_size("pole")
    z = lax.axis_index("row")
    x = lax.axis_index("col")
    pole = lax.axis_index("pole")
    _, local, _, supers, width = lower.shape
    inverse = inverse[0]
    unit = min(width, local)
    blocks = local // unit
    weights = weights[0]
    total_units = n_row * n_col * blocks
    owner = (lax.iota(jnp.int32, total_units) * unit) // width
    keep = jnp.any(pattern[:, :, None] == owner[None, None, :], axis=1).astype(jnp.int32)

    own_lower = jnp.transpose(lower[0], (2, 0, 1, 3)).reshape(supers, local, 2 * width)
    gathered = []
    for s in range(supers):
        forward = [own_lower[s]]
        backward = [own_lower[s]]
        for step in range(1, n_row):
            forward.append(lax.ppermute(forward[-1], "row", [(i, i + 1) for i in range(step - 1, n_row - 1)]))
            backward.append(lax.ppermute(backward[-1], "row", [(i, i - 1) for i in range(1, n_row - step + 1)]))
        full = jnp.zeros((n_row * local, 2 * width), lower.dtype)
        full = lax.dynamic_update_slice(full, own_lower[s], (z * local, 0))
        for d in range(1, n_row):
            piece = jnp.where(z >= d, forward[d], backward[n_row - d])
            full = lax.dynamic_update_slice(full, piece, (lax.rem(z - d + n_row, n_row) * local, 0))
        gathered.append(full)

    factors = [transposed_factor(upper[0], unit)]
    for d in range(1, n_col):
        factors.append(lax.ppermute(factors[0], "col", [(i, (i + d) % n_col) for i in range(n_col)]))
    row_total = None
    starts = []
    piece_keeps = []
    for d in range(n_col):
        origin = lax.rem(x - d + n_col, n_col)
        starts.append(origin * local)
        piece_keep = lax.dynamic_slice(keep, (0, (z * n_col + origin) * blocks), (supers, blocks))
        piece_keeps.append(piece_keep)
        meta = jnp.concatenate([(origin * blocks)[None], jnp.transpose(piece_keep).reshape(-1)])
        row_total = row_call(meta, weights, inverse, factors[d], row_total, n_row, n_pole)

    swap = [(i, n_pole - 1 - i) for i in range(n_pole)]
    mine = lax.dynamic_index_in_dim(row_total, pole, 1, keepdims=False)
    other = lax.dynamic_index_in_dim(row_total, n_pole - 1 - pole, 1, keepdims=False)
    summed = mine + lax.ppermute(other, "pole", swap)
    ahead = None
    behind = None
    for step in range(1, n_row):
        chunk = lax.dynamic_index_in_dim(summed, jnp.clip(n_row - step + z, 0, n_row - 1), 0, keepdims=False)
        send = chunk if ahead is None else chunk + ahead
        ahead = lax.ppermute(send, "row", [(i, i + 1) for i in range(0, min(step, n_row - 1))])
        chunk = lax.dynamic_index_in_dim(summed, jnp.clip(step - n_row + z, 0, n_row - 1), 0, keepdims=False)
        send = chunk if behind is None else chunk + behind
        behind = lax.ppermute(send, "row", [(i, i - 1) for i in range(n_row - step, n_row)])
    row_density = lax.dynamic_index_in_dim(summed, z, 0, keepdims=False)
    if ahead is not None:
        row_density = row_density + ahead + behind
    row_density = jnp.transpose(row_density).reshape(-1, supers, width)

    slots = n_row * blocks
    col_keep = lax.dynamic_slice(keep, (0, x * slots), (supers, slots))
    columns = []
    diagonals = []
    first_device = jnp.logical_and(z == 0, x == 0)
    given = diag_inverse[0].astype(jnp.float32)
    own_term = weights[0] * given[:, 1] + weights[1] * given[:, 0]
    own_term = jnp.where(first_device, own_term, jnp.zeros_like(own_term))
    for s in range(supers):
        count = jnp.sum(col_keep[s])
        rank = jnp.cumsum(col_keep[s]) - 1
        slot = lax.iota(jnp.int32, slots)
        wanted = jnp.minimum(slot, jnp.maximum(count - 1, 0))
        hit = jnp.logical_and(rank[None, :] == wanted[:, None], col_keep[s][None, :] > 0)
        order = jnp.sum(jnp.where(hit, slot[None, :], 0), axis=1)
        meta = jnp.concatenate(
            [count[None], order, jnp.stack(starts)] + [piece_keep[s] for piece_keep in piece_keeps]
        ).astype(jnp.int32)
        part, diag = column_call(meta, weights, inverse, gathered[s], factors, s)
        part = part.reshape(n_col, n_pole, -1, width)
        mine = lax.dynamic_index_in_dim(part, pole, 1, keepdims=False)
        other = lax.dynamic_index_in_dim(part, n_pole - 1 - pole, 1, keepdims=False)
        half = mine + lax.ppermute(other, "pole", swap)
        column = lax.dynamic_index_in_dim(half, x, 0, keepdims=False)
        for d in range(1, n_col):
            send = lax.dynamic_index_in_dim(half, lax.rem(x + d, n_col), 0, keepdims=False)
            column = column + lax.ppermute(send, "col", [(i, (i + d) % n_col) for i in range(n_col)])
        columns.append(column)
        diagonals.append(diag + own_term[s])
    column_density = jnp.stack(columns, axis=1)
    stacked = jnp.concatenate(diagonals, axis=0)
    diagonal_density = summed_everywhere(stacked, ("pole", "col", "row")).reshape(supers, width, width)
    return (column_density, row_density, diagonal_density)


def solution(mesh):
    return jax.shard_map(
        body,
        mesh=mesh,
        in_specs=(
            P(("groups", "pole"), None, "row", "col"),
            P(("groups", "pole"), ("col", "row"), None, None, None),
            P(("groups", "pole"), ("row", "col"), None, None, None),
            P(("groups", "pole"), None, None, None, None),
            P(("groups", "pole"), None),
            P("groups", None),
        ),
        out_specs=(
            P(("groups", "row", "col", "pole"), None, None),
            P(("groups", "col", "row", "pole"), None, None),
            P("groups", None, None),
        ),
        check_vma=False,
    )
```

```python
import functools

import jax
import jax.numpy as jnp
from jax import lax
from jax.experimental import pallas as pl
from jax.experimental.pallas import tpu as pltpu
from jax.sharding import PartitionSpec as P


def row_kernel(meta, weights, a_ref, u_ref, *rest):
    acc = rest[-1]
    outs = rest[-3:-1]
    previous = rest[:-3]
    k = pl.program_id(1)
    steps = pl.num_programs(1)
    supers, double, _ = acc.shape
    width = double // 2
    part = outs[0].shape[2]

    @pl.when(k == 0)
    def _():
        acc[...] = jnp.zeros_like(acc)

    for s in range(supers):
        @pl.when(meta[1 + k * supers + s] > 0)
        def _():
            real = u_ref[k, s, 0]
            imag = u_ref[k, s, 1]
            first = jnp.concatenate([real, imag], axis=0)
            second = jnp.concatenate([-imag, real], axis=0)
            acc[s] += jnp.dot(first, a_ref[0], preferred_element_type=jnp.float32) + jnp.dot(
                second, a_ref[1], preferred_element_type=jnp.float32
            )

    @pl.when(k == steps - 1)
    def _():
        for s in range(supers):
            value = -(weights[0] * acc[s, width:] + weights[1] * acc[s, :width])
            span = slice(s * width, (s + 1) * width)
            for p in range(2):
                for place in range(2):
                    @pl.when(meta[1 + steps * supers] == (p + place) % 2)
                    def _():
                        piece = value[:, p * part:(p + 1) * part]
                        if previous:
                            piece = piece + previous[place][0, span, :]
                        outs[place][0, span, :] = piece


def row_call(meta, weights, inverse, factor, prev, n_row, n_pole):
    _, _, cols = inverse.shape
    steps, supers, _, width, unit = factor.shape
    double = 2 * width
    tile = cols // n_row
    block_out = (1, supers * width, tile // n_pole)
    out_spec = pl.BlockSpec(block_out, lambda n, k, meta: (n, 0, 0))
    in_specs = [
        pl.BlockSpec(memory_space=pltpu.SMEM),
        pl.BlockSpec((2, unit, tile), lambda n, k, meta: (0, meta[0] + k, n)),
        pl.BlockSpec(factor.shape, lambda n, k, meta: (0, 0, 0, 0, 0)),
    ]
    operands = [meta, weights, inverse, factor]
    if prev is not None:
        in_specs.extend([out_spec, out_spec])
        operands.extend(prev)
    return pl.pallas_call(
        row_kernel,
        out_shape=(jax.ShapeDtypeStruct((n_row,) + block_out[1:], jnp.float32),) * 2,
        grid_spec=pltpu.PrefetchScalarGridSpec(
            num_scalar_prefetch=1,
            grid=(n_row, steps),
            in_specs=in_specs,
            out_specs=(out_spec, out_spec),
            scratch_shapes=[pltpu.VMEM((supers, double, tile), jnp.float32)],
        ),
        compiler_params=pltpu.CompilerParams(vmem_limit_bytes=56 * 2**20),
        cost_estimate=pl.CostEstimate(
            flops=4 * steps * unit * cols * supers * double // 2 * 2, bytes_accessed=4 * steps * unit * cols, transcendentals=0
        ),
        name="row_product",
    )(*operands)


def column_kernel(pieces, meta, weights, a_ref, l_ref, *rest):
    u_refs = rest[:pieces]
    mine_ref, other_ref, diag_ref, acc = rest[pieces:]
    k = pl.program_id(0)
    steps = pl.num_programs(0)
    unit, double = l_ref.shape
    width = double // 2
    parts = u_refs[0].shape[0]
    base = 2 + steps

    @pl.when(k == 0)
    def _():
        acc[...] = jnp.zeros_like(acc)

    @pl.when(k < meta[0])
    def _():
        first = l_ref[...]
        second = jnp.concatenate([-first[:, width:], first[:, :width]], axis=1)
        acc[...] += jnp.dot(a_ref[0], first, preferred_element_type=jnp.float32) + jnp.dot(
            a_ref[1], second, preferred_element_type=jnp.float32
        )

    @pl.when(k == steps - 1)
    def _():
        real = acc[:, :width]
        imag = acc[:, width:]
        mixed = weights[0] * imag + weights[1] * real
        part = mine_ref.shape[1]
        for p in range(2):
            for place, ref in enumerate((mine_ref, other_ref)):
                @pl.when(meta[base - 1] == (p + place) % 2)
                def _():
                    for c in range(mine_ref.shape[0]):
                        first_row = (2 * c + p) * part
                        ref[c] = -mixed[first_row:first_row + part]
        acc[:, width:] = weights[0] * real - weights[1] * imag
        acc[:, :width] = mixed
        diag_ref[...] = jnp.zeros_like(diag_ref)
        for i in range(pieces):
            for b in range(parts):
                @pl.when(meta[base + pieces + i * parts + b] > 0)
                def _():
                    start = pl.multiple_of(meta[base + i] + b * unit, unit)
                    value = acc[pl.ds(start, unit), :]
                    high = value.astype(jnp.bfloat16)
                    low = (value - high.astype(jnp.float32)).astype(jnp.bfloat16)
                    total = jnp.zeros(diag_ref.shape, jnp.float32)
                    for half in (high, low):
                        for c in range(2):
                            total += jnp.dot(
                                u_refs[i][b, 0, c],
                                half[:, c * width:(c + 1) * width],
                                preferred_element_type=jnp.float32,
                            )
                    diag_ref[...] += total


def column_call(meta, weights, inverse, lower, factors, s, n_col):
    _, rows, cols = inverse.shape
    double = lower.shape[1]
    width = double // 2
    parts, _, _, _, unit = factors[0].shape
    steps = cols // unit
    return pl.pallas_call(
        functools.partial(column_kernel, len(factors)),
        out_shape=(
            jax.ShapeDtypeStruct((n_col, rows // (2 * n_col), width), jnp.float32),
            jax.ShapeDtypeStruct((n_col, rows // (2 * n_col), width), jnp.float32),
            jax.ShapeDtypeStruct((width, width), jnp.float32),
        ),
        grid_spec=pltpu.PrefetchScalarGridSpec(
            num_scalar_prefetch=1,
            grid=(steps,),
            in_specs=[
                pl.BlockSpec(memory_space=pltpu.SMEM),
                pl.BlockSpec((2, rows, unit), lambda k, meta: (0, 0, meta[1 + k])),
                pl.BlockSpec((unit, double), lambda k, meta: (meta[1 + k], 0)),
            ]
            + [pl.BlockSpec((parts, 1, 2, width, unit), lambda k, meta: (0, s, 0, 0, 0))] * len(factors),
            out_specs=(
                pl.BlockSpec((n_col, rows // (2 * n_col), width), lambda k, meta: (0, 0, 0)),
                pl.BlockSpec((n_col, rows // (2 * n_col), width), lambda k, meta: (0, 0, 0)),
                pl.BlockSpec((width, width), lambda k, meta: (0, 0)),
            ),
            scratch_shapes=[pltpu.VMEM((rows, double), jnp.float32)],
        ),
        compiler_params=pltpu.CompilerParams(vmem_limit_bytes=48 * 2**20),
        cost_estimate=pl.CostEstimate(
            flops=4 * rows * cols * double // 2, bytes_accessed=2 * rows * cols, transcendentals=0
        ),
        name="column_product",
    )(meta, weights, inverse, lower, *factors)


def transposed_factor(piece, unit):
    rows, _, supers, width = piece.shape
    return jnp.transpose(piece.reshape(rows // unit, unit, 2, supers, width), (0, 3, 2, 4, 1))


def taken(array, index, axis):
    return lax.dynamic_index_in_dim(array, index, axis, keepdims=False)


def summed_everywhere(array, axes):
    if not axes:
        return array
    axis = axes[0]
    n = lax.axis_size(axis)
    me = lax.axis_index(axis)
    split = array.reshape((n, -1) + array.shape[1:])
    total = taken(split, me, 0)
    for d in range(1, n):
        pairs = [(i, (i + d) % n) for i in range(n)]
        total = total + lax.ppermute(taken(split, lax.rem(me + d, n), 0), axis, pairs)
    total = summed_everywhere(total, axes[1:])
    result = lax.dynamic_update_index_in_dim(jnp.zeros_like(split), total, me, 0)
    for d in range(1, n):
        pairs = [(i, (i + d) % n) for i in range(n)]
        got = lax.ppermute(total, axis, pairs)
        result = lax.dynamic_update_index_in_dim(result, got, lax.rem(me - d + n, n), 0)
    return result.reshape(array.shape)


def body(inverse, lower, upper, diag_inverse, weights, pattern):
    n_row = lax.axis_size("row")
    n_col = lax.axis_size("col")
    n_pole = lax.axis_size("pole")
    z = lax.axis_index("row")
    x = lax.axis_index("col")
    pole = lax.axis_index("pole")
    _, local, _, supers, width = lower.shape
    inverse = inverse[0]
    unit = min(width, local)
    blocks = local // unit
    weights = weights[0]
    total_units = n_row * n_col * blocks
    owner = (lax.iota(jnp.int32, total_units) * unit) // width
    keep = jnp.any(pattern[:, :, None] == owner[None, None, :], axis=1).astype(jnp.int32)

    own_lower = jnp.transpose(lower[0], (2, 0, 1, 3)).reshape(supers, local, 2 * width)
    chains = []
    for s in range(supers):
        forward = [own_lower[s]]
        backward = [own_lower[s]]
        for step in range(1, n_row):
            forward.append(lax.ppermute(forward[-1], "row", [(i, i + 1) for i in range(step - 1, n_row - 1)]))
            backward.append(lax.ppermute(backward[-1], "row", [(i, i - 1) for i in range(1, n_row - step + 1)]))
        chains.append((forward, backward))

    factors = [transposed_factor(upper[0], unit)]
    for d in range(1, n_col):
        factors.append(lax.ppermute(factors[0], "col", [(i, (i + d) % n_col) for i in range(n_col)]))
    row_total = None
    starts = []
    piece_keeps = []
    for d in range(n_col):
        origin = lax.rem(x - d + n_col, n_col)
        starts.append(origin * local)
        piece_keep = lax.dynamic_slice(keep, (0, (z * n_col + origin) * blocks), (supers, blocks))
        piece_keeps.append(piece_keep)
        meta = jnp.concatenate([(origin * blocks)[None], jnp.transpose(piece_keep).reshape(-1), pole[None]])
        row_total = row_call(meta, weights, inverse, factors[d], row_total, n_row, n_pole)

    swap = [(i, n_pole - 1 - i) for i in range(n_pole)]
    mine, other = row_total
    got = lax.ppermute(other, "pole", swap)

    def summed(index):
        return taken(mine, index, 0) + taken(got, index, 0)

    ahead = None
    behind = None
    for step in range(1, n_row):
        chunk = summed(jnp.clip(n_row - step + z, 0, n_row - 1))
        send = chunk if ahead is None else chunk + ahead
        ahead = lax.ppermute(send, "row", [(i, i + 1) for i in range(0, min(step, n_row - 1))])
        chunk = summed(jnp.clip(step - n_row + z, 0, n_row - 1))
        send = chunk if behind is None else chunk + behind
        behind = lax.ppermute(send, "row", [(i, i - 1) for i in range(n_row - step, n_row)])
    row_density = summed(z)
    if ahead is not None:
        row_density = row_density + ahead + behind
    row_density = jnp.transpose(row_density).reshape(-1, supers, width)

    slots = n_row * blocks
    col_keep = lax.dynamic_slice(keep, (0, x * slots), (supers, slots))
    columns = []
    diagonals = []
    first_device = jnp.logical_and(z == 0, x == 0)
    given = diag_inverse[0].astype(jnp.float32)
    own_term = weights[0] * given[:, 1] + weights[1] * given[:, 0]
    own_term = jnp.where(first_device, own_term, jnp.zeros_like(own_term))
    for s in range(supers):
        count = jnp.sum(col_keep[s])
        rank = jnp.cumsum(col_keep[s]) - 1
        slot = lax.iota(jnp.int32, slots)
        wanted = jnp.minimum(slot, jnp.maximum(count - 1, 0))
        hit = jnp.logical_and(rank[None, :] == wanted[:, None], col_keep[s][None, :] > 0)
        order = jnp.sum(jnp.where(hit, slot[None, :], 0), axis=1)
        meta = jnp.concatenate(
            [count[None], order, pole[None], jnp.stack(starts)] + [piece_keep[s] for piece_keep in piece_keeps]
        ).astype(jnp.int32)
        forward, backward = chains[s]
        last = (forward[-1], backward[-1])
        if s:
            last, diagonals[-1] = lax.optimization_barrier((last, diagonals[-1]))
        forward = forward[:-1] + [last[0]]
        backward = backward[:-1] + [last[1]]
        full = jnp.zeros((n_row * local, 2 * width), lower.dtype)
        full = lax.dynamic_update_slice(full, own_lower[s], (z * local, 0))
        for d in range(1, n_row):
            piece = jnp.where(z >= d, forward[d], backward[n_row - d])
            full = lax.dynamic_update_slice(full, piece, (lax.rem(z - d + n_row, n_row) * local, 0))
        mine, other, diag = column_call(meta, weights, inverse, full, factors, s, n_col)
        half = mine + lax.ppermute(other, "pole", swap)
        column = lax.dynamic_index_in_dim(half, x, 0, keepdims=False)
        for d in range(1, n_col):
            send = lax.dynamic_index_in_dim(half, lax.rem(x + d, n_col), 0, keepdims=False)
            column = column + lax.ppermute(send, "col", [(i, (i + d) % n_col) for i in range(n_col)])
        columns.append(column)
        diagonals.append(diag + own_term[s])
    column_density = jnp.stack(columns, axis=1)
    stacked = jnp.concatenate(diagonals, axis=0)
    diagonal_density = summed_everywhere(stacked, ("pole", "col", "row")).reshape(supers, width, width)
    return (column_density, row_density, diagonal_density)


def solution(mesh):
    return jax.shard_map(
        body,
        mesh=mesh,
        in_specs=(
            P(("groups", "pole"), None, "row", "col"),
            P(("groups", "pole"), ("col", "row"), None, None, None),
            P(("groups", "pole"), ("row", "col"), None, None, None),
            P(("groups", "pole"), None, None, None, None),
            P(("groups", "pole"), None),
            P("groups", None),
        ),
        out_specs=(
            P(("groups", "row", "col", "pole"), None, None),
            P(("groups", "col", "row", "pole"), None, None),
            P("groups", None, None),
        ),
        check_vma=False,
    )
```
